768 devices in a mesh: pipe: 32 (over x, y), seq: 24 (over z, core).
Axes of the slice: x: 4, y: 8, z: 12, core: 2. Of those that a mesh axis runs over, the one named last changes fastest.
Arguments:
- layer_input: bfloat16 [32, 1536, 2, 1536], P('pipe', 'seq'), may hold values from -1.5 to 1.5
- grad_out: bfloat16 [32, 1536, 2, 1536], P('pipe', 'seq'), may hold values from -6 to 6
- queries: bfloat16 [32, 1536, 2, 768], P('pipe', 'seq'), may hold values from -8 to 8
- keys_saved: bfloat16 [32, 1536, 2, 768], P('pipe', 'seq'), may hold values from -8 to 8
- values_saved: bfloat16 [32, 1536, 2, 768], P('pipe', 'seq'), may hold values from -6 to 6
- out_weight: bfloat16 [32, 768, 1536], P('pipe'), may hold values from -0.15625 to 0.15625
- qkv_weight: bfloat16 [32, 1536, 2304], P('pipe'), may hold values from -0.125 to 0.125
- ln_gain: bfloat16 [32, 1536], P('pipe'), may hold values from 0.099609375 to 1.8984375
- lengths: int32 [32, 2], P('pipe'), may hold values from 193 to 1536
Outputs:
- passed: bfloat16 [32, 1536, 2, 1536], P('pipe', 'seq')
The draws below stay inside these ranges and needn't reach their ends.
All inputs are finite; a program needn't handle non-finite values.
Results may differ from the reference program's by a relative error of at most 0.0063.
Values may be sent and summed in bfloat16 or wider, within the bound.
No kernel may reach another device: no remote copies, remote signals or barrier semaphores. Data moves between devices by JAX's collectives and lax.ppermute only.
A program may use at most 64 MiB of HBM per device.

```python
import jax
import jax.numpy as jnp
from jax import lax

D = 1536
HEADS_W = 12
HD = 64
RECS = 2
INNER = 768
LEN = 1536
SECTIONS = 32


def shared_projections(key):
    full_shape = (SECTIONS, LEN, RECS, INNER)
    query_vals = jnp.clip(1.5 * jax.random.normal(jax.random.fold_in(key, 1), full_shape, jnp.float32), -8.0, 8.0)
    key_vals = jnp.clip(1.5 * jax.random.normal(jax.random.fold_in(key, 2), full_shape, jnp.float32), -8.0, 8.0)
    return (query_vals, key_vals)


def draw_queries(key, part):
    return shared_projections(jax.random.fold_in(key, 11))[0].astype(jnp.bfloat16)


def draw_keys_saved(key, part):
    return shared_projections(jax.random.fold_in(key, 11))[1].astype(jnp.bfloat16)


def place_ends(entries, stream_key, low, largest):
    longest = entries.shape.index(max(entries.shape))
    spots = []
    for shift in (0, 1):
        where = [jax.random.randint(jax.random.fold_in(stream_key, axis), (), 0, length) for axis, length in enumerate(entries.shape)]
        where[longest] = (where[longest] + shift) % entries.shape[longest]
        spots.append(tuple(where))
    return entries.at[spots[0]].set(low).at[spots[1]].set(largest)


def shard_levels(stream_key, shape, split, low, largest):
    loudness, own = 1.0, jax.random.fold_in(stream_key, 6)
    for axis_at, blocks in split:
        steps = jnp.exp(jax.random.uniform(jax.random.fold_in(own, axis_at), (blocks,), jnp.float32, low / len(split), largest / len(split)))
        loudness = loudness * jnp.repeat(steps, shape[axis_at] // blocks).reshape([-1 if axis == axis_at else 1 for axis in range(len(shape))])
    return loudness


def bell_draw(stream_key, dims, deviation, most, pieces=(), kind=jnp.bfloat16):
    values = jax.random.normal(stream_key, dims, jnp.float32) * deviation
    if len(pieces) > 0:
        values = shard_levels(stream_key, dims, pieces, -0.22, 0.18) * values
    return jnp.clip(values, min=-most, max=most).astype(kind)


def setup_inputs(seed: int = 0) -> dict:
    streams_of = jax.random.split(jax.random.key(seed), 10)
    return {
        "layer_input": bell_draw(streams_of[0], (SECTIONS, LEN, RECS, D), 0.25, 1.5, ((0, 32), (1, 24))),
        "grad_out": bell_draw(streams_of[1], (SECTIONS, LEN, RECS, D), 1.0, 6.0, ((0, 32), (1, 24))),
        "queries": draw_queries(jax.random.fold_in(streams_of[9], 71), 0),
        "keys_saved": draw_keys_saved(jax.random.fold_in(streams_of[9], 71), 0),
        "values_saved": bell_draw(streams_of[4], (SECTIONS, LEN, RECS, INNER), 1.0, 6.0, ((0, 32), (1, 24))),
        "out_weight": bell_draw(streams_of[5], (SECTIONS, INNER, D), D ** -0.5, 0.15625, ((0, 32),)),
        "qkv_weight": bell_draw(streams_of[6], (SECTIONS, D, 3 * INNER), (3 * INNER) ** -0.5, 0.125, ((0, 32),)),
        "ln_gain": jnp.clip(1.0 + 0.18 * jax.random.normal(streams_of[7], (SECTIONS, D), jnp.float32), 0.099609375, 1.8984375).astype(jnp.bfloat16),
        "lengths": place_ends(jax.random.randint(streams_of[8], (SECTIONS, RECS), LEN // 8 + 1, LEN + 1), jax.random.fold_in(streams_of[8], 1), LEN // 8 + 1, LEN).astype(jnp.int32),
    }


def norm_backward(inputs, norm_gain, upstream):
    row_mean = lax.optimization_barrier(jnp.mean(inputs, axis=-1, keepdims=True))
    centred = inputs - row_mean
    row_var = lax.optimization_barrier(jnp.mean(centred * centred, axis=-1, keepdims=True))
    inv_std = lax.rsqrt(row_var + 1e-05)
    normed = centred * inv_std
    scaled = upstream * norm_gain
    return inv_std * (scaled - lax.optimization_barrier(jnp.mean(scaled, axis=-1, keepdims=True)) - normed * lax.optimization_barrier(jnp.mean(scaled * normed, axis=-1, keepdims=True)))

def one_pair(operands):
    query_rows, key_rows, value_rows, grad_rows, key_length = operands
    factor = HD ** (-0.5)
    scores = jnp.dot(query_rows, key_rows.T, preferred_element_type=jnp.float32) * factor
    usable = jnp.arange(LEN) < key_length
    masked = jnp.where(usable[None, :], scores, -jnp.inf)
    row_peak = lax.optimization_barrier(jnp.max(masked, axis=-1, keepdims=True))
    exp_terms = jnp.exp(masked - row_peak)
    prob_full = exp_terms / lax.optimization_barrier(jnp.sum(exp_terms, axis=-1, keepdims=True))
    prob_low = prob_full.astype(jnp.bfloat16)
    grad_value = jnp.dot(prob_low.T, grad_rows, preferred_element_type=jnp.float32).astype(jnp.bfloat16)
    grad_prob = jnp.dot(grad_rows, value_rows.T, preferred_element_type=jnp.float32)
    row_delta = lax.optimization_barrier(jnp.sum(prob_full * grad_prob, axis=-1, keepdims=True))
    grad_score = (prob_full * (grad_prob - row_delta)).astype(jnp.bfloat16)
    grad_query = (jnp.dot(grad_score, key_rows, preferred_element_type=jnp.float32) * factor).astype(jnp.bfloat16)
    grad_key = (jnp.dot(grad_score.T, query_rows, preferred_element_type=jnp.float32) * factor).astype(jnp.bfloat16)
    return (grad_query, grad_key, grad_value)

def section_backward(operands):
    layer_input, grad_out, queries, keys_saved, values_saved, out_weight, qkv_weight, ln_gain, lengths = operands
    row_count = LEN * RECS
    pair_count = RECS * HEADS_W
    flat_grad = grad_out.reshape(row_count, D)
    heads_grad = lax.dot_general(flat_grad, out_weight, (((1,), (1,)), ((), ())), preferred_element_type=jnp.float32).astype(jnp.bfloat16)

    def by_pair(matrix):
        return jnp.transpose(matrix.reshape(LEN, pair_count, HD), (1, 0, 2))
    key_lengths = jnp.repeat(lengths, HEADS_W)
    grad_query, grad_key, grad_value = lax.map(one_pair, (by_pair(queries), by_pair(keys_saved), by_pair(values_saved), by_pair(heads_grad), key_lengths))

    def by_frame(stacked):
        return jnp.transpose(stacked, (1, 0, 2)).reshape(row_count, INNER)
    joined = jnp.concatenate([by_frame(grad_query), by_frame(grad_key), by_frame(grad_value)], axis=1)
    grad_normed = lax.dot_general(joined, qkv_weight, (((1,), (1,)), ((), ())), preferred_element_type=jnp.float32)
    inputs = layer_input.reshape(row_count, D).astype(jnp.float32)
    branch = norm_backward(inputs, ln_gain.astype(jnp.float32)[None, :], grad_normed)
    total = flat_grad.astype(jnp.float32) + branch
    return total.astype(jnp.bfloat16).reshape(LEN, RECS, D)

def reference(layer_input, grad_out, queries, keys_saved, values_saved, out_weight, qkv_weight, ln_gain, lengths):
    grad_input = lax.map(section_backward, (layer_input, grad_out, queries, keys_saved, values_saved, out_weight, qkv_weight, ln_gain, lengths))
    return jnp.roll(grad_input, -1, axis=0)
```

```python
import jax
import jax.numpy as jnp
from jax import lax
from jax.experimental import pallas as pl
from jax.experimental.pallas import tpu as pltpu
from jax.sharding import PartitionSpec as P

HEADS_W = 12
HD = 64
LANES = 128
MASKED = -1e30
LOG2E = 1.4426950408889634
F32 = jnp.float32
BF16 = jnp.bfloat16
NT = (((1,), (1,)), ((), ()))


def passed_along(block, axis, distance):
    devices = range(lax.axis_size(axis))
    route = [((i - distance) % len(devices), i) for i in devices]
    return lax.ppermute(block, axis, route)


def low_half(shape):
    return lax.broadcasted_iota(jnp.int32, shape, len(shape) - 1) < HD


def one_hot_rows(rows, frames, records, to_interleaved):
    row = lax.broadcasted_iota(jnp.int32, (rows, rows), 0)
    col = lax.broadcasted_iota(jnp.int32, (rows, rows), 1)
    if to_interleaved:
        row, col = col, row
    hit = col == (row % frames) * records + row // frames
    return hit.astype(F32).astype(BF16)


def head_pair(left, right, low):
    turned = pltpu.roll(jnp.where(low, right, left), HD, 1)
    return jnp.where(low, left, turned), jnp.where(low, turned, right)


def pack_kernel(grad_ref, query_ref, key_ref, value_ref, weight_ref, sent_ref):
    frames, records, features = grad_ref.shape
    inner = weight_ref.shape[0]
    rows = frames * records
    order = one_hot_rows(rows, frames, records, False)

    def by_record(matrix):
        return jnp.dot(order, matrix, preferred_element_type=F32)

    flat_grad = grad_ref[...].reshape(rows, features)
    heads_grad = lax.dot_general(
        flat_grad, weight_ref[...], NT, preferred_element_type=F32
    ).astype(BF16)
    grad = by_record(heads_grad)
    query = by_record(query_ref[...].reshape(rows, inner))
    key = by_record(key_ref[...].reshape(rows, inner))
    value = by_record(value_ref[...].reshape(rows, inner))
    low = low_half((frames, LANES))
    for record in range(records):
        rs = slice(record * frames, (record + 1) * frames)
        for tile in range(inner // LANES):
            cs = slice(tile * LANES, (tile + 1) * LANES)
            pair = record * HEADS_W + 2 * tile
            qg = head_pair(query[rs, cs], grad[rs, cs], low)
            kv = head_pair(key[rs, cs], value[rs, cs], low)
            for side in range(2):
                sent_ref[pair + side, :, 0:LANES] = qg[side].astype(BF16)
                sent_ref[pair + side, :, LANES:] = kv[side].astype(BF16)


def attend_kernel(
    length_ref, heads_ref, back_ref, kt_ref, q_ref, g_ref, bias_ref, score_ref, prob_ref, acc_ref
):
    length = heads_ref.shape[0]
    devices, packed, _ = back_ref.shape
    frames = length // devices
    block = 256
    chunks = length // block
    record = lax.axis_index("seq") // HEADS_W
    key_length = jnp.where(record == 0, length_ref[0, 0], length_ref[0, 1])
    factor = HD ** (-0.5)
    rate = factor * LOG2E

    low = low_half((length, LANES))
    both = heads_ref[:, 0:LANES].astype(F32)
    q_ref[...] = jnp.where(low, both, 0.0).astype(BF16)
    g_ref[...] = jnp.where(low, 0.0, both).astype(BF16)
    kt_ref[...] = heads_ref[:, LANES:].astype(F32).T[0:HD].astype(BF16)
    bias_ref[...] = jnp.where(
        lax.broadcasted_iota(jnp.int32, (length, LANES), 0) < key_length, 0.0, MASKED
    )

    def fold(values, op):
        return op(values.reshape(-1, 8, block), axis=0)

    for qb in range(chunks):
        qs = slice(qb * block, (qb + 1) * block)
        q_blk = q_ref[qs, :]
        g_blk = g_ref[qs, :]
        peak = None
        for c in range(chunks):
            ks = slice(c * block, (c + 1) * block)
            bias = bias_ref[ks, :]
            scores = lax.dot_general(
                heads_ref[ks, LANES:], q_blk, NT, preferred_element_type=F32
            ) + jnp.concatenate([bias] * (block // LANES), axis=1)
            score_ref[ks, :] = scores
            part = fold(scores, jnp.max)
            peak = part if peak is None else jnp.maximum(peak, part)
        peak = jnp.max(peak, axis=0, keepdims=True)
        total = None
        weighted = None
        for c in range(chunks):
            ks = slice(c * block, (c + 1) * block)
            terms = jnp.exp2((score_ref[ks, :] - peak) * rate)
            grad_prob = lax.dot_general(
                heads_ref[ks, LANES:], g_blk, NT, preferred_element_type=F32
            )
            score_ref[ks, :] = terms
            prob_ref[ks, :] = grad_prob
            part = fold(terms, jnp.sum)
            total = part if total is None else total + part
            part = fold(terms * grad_prob, jnp.sum)
            weighted = part if weighted is None else weighted + part
        share = 1.0 / jnp.sum(total, axis=0, keepdims=True)
        delta = jnp.sum(weighted, axis=0, keepdims=True) * share
        grad_q = None
        for c in range(chunks):
            ks = slice(c * block, (c + 1) * block)
            prob = score_ref[ks, :] * share
            grad_score = (prob * (prob_ref[ks, :] - delta)).astype(BF16)
            update = jnp.dot(prob.astype(BF16), g_blk, preferred_element_type=F32) + jnp.dot(
                grad_score, q_blk, preferred_element_type=F32
            )
            if qb == 0:
                acc_ref[ks, :] = update
            else:
                acc_ref[ks, :] += update
            part = jnp.dot(kt_ref[:, ks], grad_score, preferred_element_type=F32)
            grad_q = part if grad_q is None else grad_q + part
        rows = (grad_q.T * factor).reshape(block // frames, frames, HD)
        half = frames // 2
        for j in range(block // frames):
            back_ref[qb * (block // frames) + j, frames:packed, :] = jnp.concatenate(
                [rows[j, 0:half], rows[j, half:]], axis=1
            ).astype(BF16)
    scale = jnp.where(low_half((1, LANES)), factor, 1.0)
    back_ref[:, 0:frames, :] = (acc_ref[...] * scale).astype(BF16).reshape(devices, frames, LANES)


def finish_kernel(back_ref, weight_ref, input_ref, grad_ref, gain_ref, out_ref, joined_ref):
    frames, records, features = grad_ref.shape
    rows = frames * records
    inner = weight_ref.shape[1] // 3
    half = frames // 2
    low = low_half((frames, LANES))
    low_part = low_half((half, LANES))
    for record in range(records):
        base = record * frames
        for tile in range(inner // LANES):
            pair = record * HEADS_W + 2 * tile
            first = back_ref[pair].astype(F32)
            second = back_ref[pair + 1].astype(F32)
            key, value = head_pair(first[0:frames], second[0:frames], low)
            upper, lower = head_pair(first[frames:], second[frames:], low_part)
            cs = tile * LANES
            joined_ref[base : base + half, cs : cs + LANES] = upper.astype(BF16)
            joined_ref[base + half : base + frames, cs : cs + LANES] = lower.astype(BF16)
            joined_ref[base : base + frames, inner + cs : inner + cs + LANES] = key.astype(BF16)
            joined_ref[base : base + frames, 2 * inner + cs : 2 * inner + cs + LANES] = (
                value.astype(BF16)
            )
    order = one_hot_rows(rows, frames, records, True)
    joined = jnp.dot(order, joined_ref[...], preferred_element_type=F32).astype(BF16)
    upstream = lax.dot_general(joined, weight_ref[...], NT, preferred_element_type=F32)
    inputs = input_ref[...].reshape(rows, features).astype(F32)
    row_mean = jnp.mean(inputs, axis=-1, keepdims=True)
    centred = inputs - row_mean
    row_var = jnp.mean(centred * centred, axis=-1, keepdims=True)
    inv_std = lax.rsqrt(row_var + 1e-05)
    normed = centred * inv_std
    scaled = upstream * gain_ref[...].astype(F32)
    branch = inv_std * (
        scaled
        - jnp.mean(scaled, axis=-1, keepdims=True)
        - normed * jnp.mean(scaled * normed, axis=-1, keepdims=True)
    )
    total = grad_ref[...].reshape(rows, features).astype(F32) + branch
    out_ref[...] = total.astype(BF16).reshape(frames, records, features)


def per_device(
    layer_input,
    grad_out,
    queries,
    keys_saved,
    values_saved,
    out_weight,
    qkv_weight,
    ln_gain,
    lengths,
):
    frames, records, features = grad_out.shape[1:]
    inner = out_weight.shape[1]
    devices = lax.axis_size("seq")
    length = devices * frames
    packed = frames + frames // 2
    block = 256
    vmem = pltpu.CompilerParams(vmem_limit_bytes=48 * 1024 * 1024)

    sent = pl.pallas_call(
        pack_kernel,
        out_shape=jax.ShapeDtypeStruct((devices, frames, 2 * LANES), BF16),
        compiler_params=vmem,
        name="pack",
    )(grad_out[0], queries[0], keys_saved[0], values_saved[0], out_weight[0])
    heads = lax.all_to_all(sent, "seq", split_axis=0, concat_axis=0, tiled=True)
    whole = pl.BlockSpec(memory_space=pltpu.VMEM)
    back = pl.pallas_call(
        attend_kernel,
        out_shape=jax.ShapeDtypeStruct((devices, packed, LANES), BF16),
        in_specs=[pl.BlockSpec(memory_space=pltpu.SMEM), whole],
        out_specs=whole,
        scratch_shapes=[
            pltpu.VMEM((HD, length), BF16),
            pltpu.VMEM((length, LANES), BF16),
            pltpu.VMEM((length, LANES), BF16),
            pltpu.VMEM((length, LANES), F32),
            pltpu.VMEM((length, block), F32),
            pltpu.VMEM((length, block), F32),
            pltpu.VMEM((length, LANES), F32),
        ],
        compiler_params=vmem,
        name="attend",
    )(lengths, heads.reshape(length, 2 * LANES))
    back = lax.all_to_all(back, "seq", split_axis=0, concat_axis=0, tiled=True)
    total = pl.pallas_call(
        finish_kernel,
        out_shape=jax.ShapeDtypeStruct((frames, records, features), BF16),
        scratch_shapes=[pltpu.VMEM((frames * records, 3 * inner), BF16)],
        compiler_params=vmem,
        name="finish",
    )(back, qkv_weight[0], layer_input[0], grad_out[0], ln_gain)
    return passed_along(total, "pipe", -1)[None]


def solution(mesh):
    placed = (
        P("pipe", "seq", None, None),
        P("pipe", "seq", None, None),
        P("pipe", "seq", None, None),
        P("pipe", "seq", None, None),
        P("pipe", "seq", None, None),
        P("pipe", None, None),
        P("pipe", None, None),
        P("pipe", None),
        P("pipe", None),
    )
    return jax.shard_map(
        per_device,
        mesh=mesh,
        in_specs=placed,
        out_specs=P("pipe", "seq", None, None),
        check_vma=False,
    )
```

```python
import jax
import jax.numpy as jnp
from jax import lax
from jax.experimental import pallas as pl
from jax.experimental.pallas import tpu as pltpu
from jax.sharding import PartitionSpec as P

HEADS_W = 12
HD = 64
LANES = 128
MASKED = -1e30
LOG2E = 1.4426950408889634
F32 = jnp.float32
BF16 = jnp.bfloat16
NT = (((1,), (1,)), ((), ()))


def passed_along(block, axis, distance):
    devices = range(lax.axis_size(axis))
    route = [((i - distance) % len(devices), i) for i in devices]
    return lax.ppermute(block, axis, route)


def low_half(shape):
    return lax.broadcasted_iota(jnp.int32, shape, len(shape) - 1) < HD


def one_hot_rows(rows, frames, records, to_interleaved):
    row = lax.broadcasted_iota(jnp.int32, (rows, rows), 0)
    col = lax.broadcasted_iota(jnp.int32, (rows, rows), 1)
    if to_interleaved:
        row, col = col, row
    hit = col == (row % frames) * records + row // frames
    return hit.astype(F32).astype(BF16)


def head_pair(left, right, low):
    turned = pltpu.roll(jnp.where(low, right, left), HD, 1)
    return jnp.where(low, left, turned), jnp.where(low, turned, right)


def pack_kernel(
    grad_hbm,
    query_hbm,
    key_hbm,
    value_hbm,
    weight_hbm,
    sent_ref,
    grad_ref,
    query_ref,
    key_ref,
    value_ref,
    weight_ref,
    sems,
):
    frames, records, features = grad_ref.shape
    inner = weight_ref.shape[0]
    rows = frames * records
    loads = [
        pltpu.make_async_copy(source, target, sems.at[n])
        for n, (source, target) in enumerate(
            (
                (key_hbm, key_ref),
                (value_hbm, value_ref),
                (grad_hbm, grad_ref),
                (query_hbm, query_ref),
                (weight_hbm, weight_ref),
            )
        )
    ]
    for load in loads:
        load.start()
    order = one_hot_rows(rows, frames, records, False)

    def by_record(matrix):
        return jnp.dot(order, matrix, preferred_element_type=F32)

    low = low_half((frames, LANES))

    def place(first, second, start):
        for record in range(records):
            rs = slice(record * frames, (record + 1) * frames)
            for tile in range(inner // LANES):
                cs = slice(tile * LANES, (tile + 1) * LANES)
                pair = record * HEADS_W + 2 * tile
                sides = head_pair(first[rs, cs], second[rs, cs], low)
                for side in range(2):
                    sent_ref[pair + side, :, start : start + LANES] = sides[side].astype(BF16)

    loads[0].wait()
    loads[1].wait()
    key = by_record(key_ref[...].reshape(rows, inner))
    value = by_record(value_ref[...].reshape(rows, inner))
    place(key, value, LANES)
    for load in loads[2:]:
        load.wait()
    query = by_record(query_ref[...].reshape(rows, inner))
    flat_grad = grad_ref[...].reshape(rows, features)
    heads_grad = lax.dot_general(
        flat_grad, weight_ref[...], NT, preferred_element_type=F32
    ).astype(BF16)
    place(query, by_record(heads_grad), 0)


def attend_kernel(
    length_hbm,
    heads_ref,
    back_ref,
    kt_ref,
    q_ref,
    g_ref,
    bias_ref,
    score_ref,
    prob_ref,
    acc_ref,
    length_ref,
    sem,
):
    load = pltpu.make_async_copy(length_hbm, length_ref, sem)
    load.start()
    length = heads_ref.shape[0]
    devices, packed, _ = back_ref.shape
    frames = length // devices
    block = 256
    chunks = length // block
    factor = HD ** (-0.5)
    rate = factor * LOG2E

    low = low_half((length, LANES))
    both = heads_ref[:, 0:LANES].astype(F32)
    q_ref[...] = jnp.where(low, both, 0.0).astype(BF16)
    g_ref[...] = jnp.where(low, 0.0, both).astype(BF16)
    kt_ref[...] = heads_ref[:, LANES:].astype(F32).T[0:HD].astype(BF16)
    load.wait()
    record = lax.axis_index("seq") // HEADS_W
    key_length = jnp.where(record == 0, length_ref[0, 0], length_ref[0, 1])
    bias_ref[...] = jnp.where(
        lax.broadcasted_iota(jnp.int32, (length, LANES), 0) < key_length, 0.0, MASKED
    )

    def fold(values, op):
        return op(values.reshape(-1, 8, block), axis=0)

    for qb in range(chunks):
        qs = slice(qb * block, (qb + 1) * block)
        q_blk = q_ref[qs, :]
        g_blk = g_ref[qs, :]
        peak = None
        for c in range(chunks):
            ks = slice(c * block, (c + 1) * block)
            bias = bias_ref[ks, :]
            scores = lax.dot_general(
                heads_ref[ks, LANES:], q_blk, NT, preferred_element_type=F32
            ) + jnp.concatenate([bias] * (block // LANES), axis=1)
            score_ref[ks, :] = scores
            part = fold(scores, jnp.max)
            peak = part if peak is None else jnp.maximum(peak, part)
        peak = jnp.max(peak, axis=0, keepdims=True)
        total = None
        weighted = None
        for c in range(chunks):
            ks = slice(c * block, (c + 1) * block)
            terms = jnp.exp2((score_ref[ks, :] - peak) * rate)
            grad_prob = lax.dot_general(
                heads_ref[ks, LANES:], g_blk, NT, preferred_element_type=F32
            )
            score_ref[ks, :] = terms
            prob_ref[ks, :] = grad_prob
            part = fold(terms, jnp.sum)
            total = part if total is None else total + part
            part = fold(terms * grad_prob, jnp.sum)
            weighted = part if weighted is None else weighted + part
        share = 1.0 / jnp.sum(total, axis=0, keepdims=True)
        delta = jnp.sum(weighted, axis=0, keepdims=True) * share
        grad_q = None
        for c in range(chunks):
            ks = slice(c * block, (c + 1) * block)
            prob = score_ref[ks, :] * share
            grad_score = (prob * (prob_ref[ks, :] - delta)).astype(BF16)
            update = jnp.dot(prob.astype(BF16), g_blk, preferred_element_type=F32) + jnp.dot(
                grad_score, q_blk, preferred_element_type=F32
            )
            if qb == 0:
                acc_ref[ks, :] = update
            else:
                acc_ref[ks, :] += update
            part = jnp.dot(kt_ref[:, ks], grad_score, preferred_element_type=F32)
            grad_q = part if grad_q is None else grad_q + part
        rows = (grad_q.T * factor).reshape(block // frames, frames, HD)
        half = frames // 2
        for j in range(block // frames):
            back_ref[qb * (block // frames) + j, frames:packed, :] = jnp.concatenate(
                [rows[j, 0:half], rows[j, half:]], axis=1
            ).astype(BF16)
    scale = jnp.where(low_half((1, LANES)), factor, 1.0)
    back_ref[:, 0:frames, :] = (acc_ref[...] * scale).astype(BF16).reshape(devices, frames, LANES)


def finish_kernel(back_ref, weight_ref, input_ref, grad_ref, gain_ref, out_ref, joined_ref):
    frames, records, features = grad_ref.shape
    rows = frames * records
    inner = weight_ref.shape[1] // 3
    half = frames // 2
    low = low_half((frames, LANES))
    low_part = low_half((half, LANES))
    for record in range(records):
        base = record * frames
        for tile in range(inner // LANES):
            pair = record * HEADS_W + 2 * tile
            first = back_ref[pair].astype(F32)
            second = back_ref[pair + 1].astype(F32)
            key, value = head_pair(first[0:frames], second[0:frames], low)
            upper, lower = head_pair(first[frames:], second[frames:], low_part)
            cs = tile * LANES
            joined_ref[base : base + half, cs : cs + LANES] = upper.astype(BF16)
            joined_ref[base + half : base + frames, cs : cs + LANES] = lower.astype(BF16)
            joined_ref[base : base + frames, inner + cs : inner + cs + LANES] = key.astype(BF16)
            joined_ref[base : base + frames, 2 * inner + cs : 2 * inner + cs + LANES] = (
                value.astype(BF16)
            )
    order = one_hot_rows(rows, frames, records, True)
    joined = jnp.dot(order, joined_ref[...], preferred_element_type=F32).astype(BF16)
    upstream = lax.dot_general(joined, weight_ref[...], NT, preferred_element_type=F32)
    inputs = input_ref[...].reshape(rows, features).astype(F32)
    row_mean = jnp.mean(inputs, axis=-1, keepdims=True)
    centred = inputs - row_mean
    row_var = jnp.mean(centred * centred, axis=-1, keepdims=True)
    inv_std = lax.rsqrt(row_var + 1e-05)
    normed = centred * inv_std
    scaled = upstream * gain_ref[...].astype(F32)
    branch = inv_std * (
        scaled
        - jnp.mean(scaled, axis=-1, keepdims=True)
        - normed * jnp.mean(scaled * normed, axis=-1, keepdims=True)
    )
    total = grad_ref[...].reshape(rows, features).astype(F32) + branch
    out_ref[...] = total.astype(BF16).reshape(frames, records, features)


def per_device(
    layer_input,
    grad_out,
    queries,
    keys_saved,
    values_saved,
    out_weight,
    qkv_weight,
    ln_gain,
    lengths,
):
    frames, records, features = grad_out.shape[1:]
    inner = out_weight.shape[1]
    devices = lax.axis_size("seq")
    length = devices * frames
    packed = frames + frames // 2
    block = 256
    vmem = pltpu.CompilerParams(vmem_limit_bytes=24 * 1024 * 1024)
    far = pl.BlockSpec(memory_space=pltpu.HBM)
    whole = pl.BlockSpec(memory_space=pltpu.VMEM)

    sent = pl.pallas_call(
        pack_kernel,
        out_shape=jax.ShapeDtypeStruct((devices, frames, 2 * LANES), BF16),
        in_specs=[far] * 5,
        out_specs=whole,
        scratch_shapes=[
            pltpu.VMEM((frames, records, features), BF16),
            pltpu.VMEM((frames, records, inner), BF16),
            pltpu.VMEM((frames, records, inner), BF16),
            pltpu.VMEM((frames, records, inner), BF16),
            pltpu.VMEM((inner, features), BF16),
            pltpu.SemaphoreType.DMA((5,)),
        ],
        compiler_params=vmem,
        name="pack",
    )(
        *(
            pltpu.with_memory_space_constraint(array[0], pltpu.HBM)
            for array in (grad_out, queries, keys_saved, values_saved, out_weight)
        )
    )
    heads = lax.all_to_all(sent, "seq", split_axis=0, concat_axis=0, tiled=True)
    back = pl.pallas_call(
        attend_kernel,
        out_shape=jax.ShapeDtypeStruct((devices, packed, LANES), BF16),
        in_specs=[far, whole],
        out_specs=whole,
        scratch_shapes=[
            pltpu.VMEM((HD, length), BF16),
            pltpu.VMEM((length, LANES), BF16),
            pltpu.VMEM((length, LANES), BF16),
            pltpu.VMEM((length, LANES), F32),
            pltpu.VMEM((length, block), F32),
            pltpu.VMEM((length, block), F32),
            pltpu.VMEM((length, LANES), F32),
            pltpu.SMEM(lengths.shape, jnp.int32),
            pltpu.SemaphoreType.DMA,
        ],
        compiler_params=vmem,
        name="attend",
    )(pltpu.with_memory_space_constraint(lengths, pltpu.HBM), heads.reshape(length, 2 * LANES))
    back = lax.all_to_all(back, "seq", split_axis=0, concat_axis=0, tiled=True)
    total = pl.pallas_call(
        finish_kernel,
        out_shape=jax.ShapeDtypeStruct((frames, records, features), BF16),
        scratch_shapes=[pltpu.VMEM((frames * records, 3 * inner), BF16)],
        compiler_params=vmem,
        name="finish",
    )(back, qkv_weight[0], layer_input[0], grad_out[0], ln_gain)
    return passed_along(total, "pipe", -1)[None]


def solution(mesh):
    placed = (
        P("pipe", "seq", None, None),
        P("pipe", "seq", None, None),
        P("pipe", "seq", None, None),
        P("pipe", "seq", None, None),
        P("pipe", "seq", None, None),
        P("pipe", None, None),
        P("pipe", None, None),
        P("pipe", None),
        P("pipe", None),
    )
    return jax.shard_map(
        per_device,
        mesh=mesh,
        in_specs=placed,
        out_specs=P("pipe", "seq", None, None),
        check_vma=False,
    )
```

```python
import jax
import jax.numpy as jnp
from jax import lax
from jax.experimental import pallas as pl
from jax.experimental.pallas import tpu as pltpu
from jax.sharding import PartitionSpec as P

HEADS_W = 12
HD = 64
LANES = 128
MASKED = -1e30
LOG2E = 1.4426950408889634
F32 = jnp.float32
BF16 = jnp.bfloat16
NT = (((1,), (1,)), ((), ()))


def passed_along(block, axis, distance):
    devices = range(lax.axis_size(axis))
    route = [((i - distance) % len(devices), i) for i in devices]
    return lax.ppermute(block, axis, route)


def low_half(shape):
    return lax.broadcasted_iota(jnp.int32, shape, len(shape) - 1) < HD


def one_hot_rows(rows, frames, records, to_interleaved):
    row = lax.broadcasted_iota(jnp.int32, (rows, rows), 0)
    col = lax.broadcasted_iota(jnp.int32, (rows, rows), 1)
    if to_interleaved:
        row, col = col, row
    hit = col == (row % frames) * records + row // frames
    return hit.astype(F32).astype(BF16)


def head_pair(left, right, low):
    turned = pltpu.roll(jnp.where(low, right, left), HD, 1)
    return jnp.where(low, left, turned), jnp.where(low, turned, right)


def pack_kernel(
    grad_hbm,
    query_hbm,
    key_hbm,
    value_hbm,
    weight_hbm,
    sent_ref,
    grad_ref,
    query_ref,
    key_ref,
    value_ref,
    weight_ref,
    sems,
):
    frames, records, features = grad_ref.shape
    inner = weight_ref.shape[0]
    rows = frames * records
    loads = [
        pltpu.make_async_copy(source, target, sems.at[n])
        for n, (source, target) in enumerate(
            (
                (key_hbm, key_ref),
                (value_hbm, value_ref),
                (grad_hbm, grad_ref),
                (query_hbm, query_ref),
                (weight_hbm, weight_ref),
            )
        )
    ]
    for load in loads:
        load.start()
    order = one_hot_rows(rows, frames, records, False)

    def by_record(matrix):
        return jnp.dot(order, matrix, preferred_element_type=F32)

    low = low_half((frames, LANES))

    def place(first, second, start):
        for record in range(records):
            rs = slice(record * frames, (record + 1) * frames)
            for tile in range(inner // LANES):
                cs = slice(tile * LANES, (tile + 1) * LANES)
                pair = record * HEADS_W + 2 * tile
                sides = head_pair(first[rs, cs], second[rs, cs], low)
                for side in range(2):
                    sent_ref[pair + side, :, start : start + LANES] = sides[side].astype(BF16)

    loads[0].wait()
    loads[1].wait()
    key = by_record(key_ref[...].reshape(rows, inner))
    value = by_record(value_ref[...].reshape(rows, inner))
    place(key, value, LANES)
    for load in loads[2:]:
        load.wait()
    query = by_record(query_ref[...].reshape(rows, inner))
    flat_grad = grad_ref[...].reshape(rows, features)
    heads_grad = lax.dot_general(
        flat_grad, weight_ref[...], NT, preferred_element_type=F32
    ).astype(BF16)
    place(query, by_record(heads_grad), 0)


def attend_kernel(
    length_hbm,
    heads_ref,
    back_ref,
    kt_ref,
    gq_ref,
    bias_ref,
    terms_ref,
    prob_ref,
    acc_ref,
    length_ref,
    sem,
):
    load = pltpu.make_async_copy(length_hbm, length_ref, sem)
    load.start()
    length = heads_ref.shape[0]
    devices, packed, _ = back_ref.shape
    frames = length // devices
    block = terms_ref.shape[2]
    chunk = 128
    factor = HD ** (-0.5)
    rate = factor * LOG2E

    low = low_half((length, LANES))
    both = heads_ref[:, 0:LANES].astype(F32)
    only_g = jnp.where(low, 0.0, both).astype(BF16)
    only_q = jnp.where(low, both, 0.0).astype(BF16)
    for qb in range(length // block):
        rows = slice(qb * block, (qb + 1) * block)
        gq_ref[2 * qb * block : (2 * qb + 1) * block, :] = only_g[rows]
        gq_ref[(2 * qb + 1) * block : (2 * qb + 2) * block, :] = only_q[rows]
    kt_ref[...] = heads_ref[:, LANES:].astype(F32).T[0:HD].astype(BF16)
    load.wait()
    record = lax.axis_index("seq") // HEADS_W
    key_length = jnp.where(record == 0, length_ref[0, 0], length_ref[0, 1])
    bias_ref[...] = jnp.where(
        lax.broadcasted_iota(jnp.int32, (length, LANES), 0) < key_length, 0.0, MASKED
    )

    def fold(values, op):
        return op(values.reshape(-1, 8, block), axis=0)

    def first_stage(qb, c, state):
        ks = slice(c * chunk, (c + 1) * chunk)
        g_blk = gq_ref[2 * qb * block : (2 * qb + 1) * block, :]
        q_blk = gq_ref[(2 * qb + 1) * block : (2 * qb + 2) * block, :]
        bias = jnp.concatenate([bias_ref[ks, :]] * (block // LANES), axis=1)
        scores = (
            lax.dot_general(heads_ref[ks, LANES:], q_blk, NT, preferred_element_type=F32) + bias
        )
        peak = jnp.max(fold(scores, jnp.max), axis=0, keepdims=True)
        terms = jnp.exp2((scores - peak) * rate)
        grad_prob = lax.dot_general(
            heads_ref[ks, LANES:], g_blk, NT, preferred_element_type=F32
        )
        terms_ref[qb % 2, ks, :] = terms
        prob_ref[qb % 2, ks, :] = grad_prob
        state["peaks"].append(peak)
        state["sums"].append(fold(terms, jnp.sum))
        state["weighted"].append(fold(terms * grad_prob, jnp.sum))

    def row_totals(state):
        top = state["peaks"][0]
        for peak in state["peaks"][1:]:
            top = jnp.maximum(top, peak)
        scales = [jnp.exp2((peak - top) * rate) for peak in state["peaks"]]
        total = sum(part * scale for part, scale in zip(state["sums"], scales))
        weighted = sum(part * scale for part, scale in zip(state["weighted"], scales))
        share = 1.0 / jnp.sum(total, axis=0, keepdims=True)
        state["delta"] = jnp.sum(weighted, axis=0, keepdims=True) * share
        state["shares"] = [share * scale for scale in scales]
        state["grad_q"] = 0.0

    def last_stage(qb, c, state):
        ks = slice(c * chunk, (c + 1) * chunk)
        prob = terms_ref[qb % 2, ks, :] * state["shares"][c]
        grad_score = (prob * (prob_ref[qb % 2, ks, :] - state["delta"])).astype(BF16)
        update = jnp.dot(
            jnp.concatenate([prob.astype(BF16), grad_score], axis=1),
            gq_ref[2 * qb * block : (2 * qb + 2) * block, :],
            preferred_element_type=F32,
        )
        if qb == 0:
            acc_ref[ks, :] = update
        else:
            acc_ref[ks, :] += update
        state["grad_q"] = state["grad_q"] + jnp.dot(
            kt_ref[:, ks], grad_score, preferred_element_type=F32
        )

    def send_queries(qb, state):
        rows = (state["grad_q"].T * factor).reshape(block // frames, frames, HD)
        half = frames // 2
        for j in range(block // frames):
            back_ref[qb * (block // frames) + j, frames:packed, :] = jnp.concatenate(
                [rows[j, 0:half], rows[j, half:]], axis=1
            ).astype(BF16)

    blocks = length // block
    states = [dict(peaks=[], sums=[], weighted=[]) for _ in range(blocks)]
    for qb in range(blocks + 1):
        for c in range(length // chunk):
            if qb < blocks:
                first_stage(qb, c, states[qb])
            if qb > 0:
                last_stage(qb - 1, c, states[qb - 1])
        if qb < blocks:
            row_totals(states[qb])
        if qb > 0:
            send_queries(qb - 1, states[qb - 1])
    scale = jnp.where(low_half((1, LANES)), factor, 1.0)
    back_ref[:, 0:frames, :] = (acc_ref[...] * scale).astype(BF16).reshape(devices, frames, LANES)


def finish_kernel(back_ref, weight_ref, input_ref, grad_ref, gain_ref, out_ref, joined_ref):
    frames, records, features = grad_ref.shape
    rows = frames * records
    inner = weight_ref.shape[1] // 3
    half = frames // 2
    low = low_half((frames, LANES))
    low_part = low_half((half, LANES))
    for record in range(records):
        base = record * frames
        for tile in range(inner // LANES):
            pair = record * HEADS_W + 2 * tile
            first = back_ref[pair].astype(F32)
            second = back_ref[pair + 1].astype(F32)
            key, value = head_pair(first[0:frames], second[0:frames], low)
            upper, lower = head_pair(first[frames:], second[frames:], low_part)
            cs = tile * LANES
            joined_ref[base : base + half, cs : cs + LANES] = upper.astype(BF16)
            joined_ref[base + half : base + frames, cs : cs + LANES] = lower.astype(BF16)
            joined_ref[base : base + frames, inner + cs : inner + cs + LANES] = key.astype(BF16)
            joined_ref[base : base + frames, 2 * inner + cs : 2 * inner + cs + LANES] = (
                value.astype(BF16)
            )
    order = one_hot_rows(rows, frames, records, True)
    joined = jnp.dot(order, joined_ref[...], preferred_element_type=F32).astype(BF16)
    upstream = lax.dot_general(joined, weight_ref[...], NT, preferred_element_type=F32)
    inputs = input_ref[...].reshape(rows, features).astype(F32)
    row_mean = jnp.mean(inputs, axis=-1, keepdims=True)
    centred = inputs - row_mean
    row_var = jnp.mean(centred * centred, axis=-1, keepdims=True)
    inv_std = lax.rsqrt(row_var + 1e-05)
    normed = centred * inv_std
    scaled = upstream * gain_ref[...].astype(F32)
    branch = inv_std * (
        scaled
        - jnp.mean(scaled, axis=-1, keepdims=True)
        - normed * jnp.mean(scaled * normed, axis=-1, keepdims=True)
    )
    total = grad_ref[...].reshape(rows, features).astype(F32) + branch
    out_ref[...] = total.astype(BF16).reshape(frames, records, features)


def per_device(
    layer_input,
    grad_out,
    queries,
    keys_saved,
    values_saved,
    out_weight,
    qkv_weight,
    ln_gain,
    lengths,
):
    frames, records, features = grad_out.shape[1:]
    inner = out_weight.shape[1]
    devices = lax.axis_size("seq")
    length = devices * frames
    packed = frames + frames // 2
    block = 256
    vmem = pltpu.CompilerParams(vmem_limit_bytes=24 * 1024 * 1024)
    far = pl.BlockSpec(memory_space=pltpu.HBM)
    whole = pl.BlockSpec(memory_space=pltpu.VMEM)

    sent = pl.pallas_call(
        pack_kernel,
        out_shape=jax.ShapeDtypeStruct((devices, frames, 2 * LANES), BF16),
        in_specs=[far] * 5,
        out_specs=whole,
        scratch_shapes=[
            pltpu.VMEM((frames, records, features), BF16),
            pltpu.VMEM((frames, records, inner), BF16),
            pltpu.VMEM((frames, records, inner), BF16),
            pltpu.VMEM((frames, records, inner), BF16),
            pltpu.VMEM((inner, features), BF16),
            pltpu.SemaphoreType.DMA((5,)),
        ],
        compiler_params=pltpu.CompilerParams(vmem_limit_bytes=50 * 1024 * 1024),
        name="pack",
    )(
        *(
            pltpu.with_memory_space_constraint(array[0], pltpu.HBM)
            for array in (grad_out, queries, keys_saved, values_saved, out_weight)
        )
    )
    heads = lax.all_to_all(sent, "seq", split_axis=0, concat_axis=0, tiled=True)
    back = pl.pallas_call(
        attend_kernel,
        out_shape=jax.ShapeDtypeStruct((devices, packed, LANES), BF16),
        in_specs=[far, whole],
        out_specs=whole,
        scratch_shapes=[
            pltpu.VMEM((HD, length), BF16),
            pltpu.VMEM((2 * length, LANES), BF16),
            pltpu.VMEM((length, LANES), F32),
            pltpu.VMEM((2, length, block), F32),
            pltpu.VMEM((2, length, block), F32),
            pltpu.VMEM((length, LANES), F32),
            pltpu.SMEM(lengths.shape, jnp.int32),
            pltpu.SemaphoreType.DMA,
        ],
        compiler_params=vmem,
        cost_estimate=pl.CostEstimate(
            flops=64 * length * length * HD,
            bytes_accessed=8 * length * LANES,
            transcendentals=length * length,
        ),
        name="attend",
    )(pltpu.with_memory_space_constraint(lengths, pltpu.HBM), heads.reshape(length, 2 * LANES))
    back = lax.all_to_all(back, "seq", split_axis=0, concat_axis=0, tiled=True)
    total = pl.pallas_call(
        finish_kernel,
        out_shape=jax.ShapeDtypeStruct((frames, records, features), BF16),
        scratch_shapes=[pltpu.VMEM((frames * records, 3 * inner), BF16)],
        compiler_params=vmem,
        name="finish",
    )(back, qkv_weight[0], layer_input[0], grad_out[0], ln_gain)
    return passed_along(total, "pipe", -1)[None]


def solution(mesh):
    placed = (
        P("pipe", "seq", None, None),
        P("pipe", "seq", None, None),
        P("pipe", "seq", None, None),
        P("pipe", "seq", None, None),
        P("pipe", "seq", None, None),
        P("pipe", None, None),
        P("pipe", None, None),
        P("pipe", None),
        P("pipe", None),
    )
    return jax.shard_map(
        per_device,
        mesh=mesh,
        in_specs=placed,
        out_specs=P("pipe", "seq", None, None),
        check_vma=False,
    )
```

```python
import jax
import jax.numpy as jnp
from jax import lax
from jax.experimental import pallas as pl
from jax.experimental.pallas import tpu as pltpu
from jax.sharding import PartitionSpec as P

HEADS_W = 12
HD = 64
LANES = 128
MASKED = -1e30
LOG2E = 1.4426950408889634
F32 = jnp.float32
BF16 = jnp.bfloat16
NT = (((1,), (1,)), ((), ()))


def passed_along(block, axis, distance):
    devices = range(lax.axis_size(axis))
    route = [((i - distance) % len(devices), i) for i in devices]
    return lax.ppermute(block, axis, route)


def low_half(shape):
    return lax.broadcasted_iota(jnp.int32, shape, len(shape) - 1) < HD


def one_hot_rows(rows, frames, records, to_interleaved):
    row = lax.broadcasted_iota(jnp.int32, (rows, rows), 0)
    col = lax.broadcasted_iota(jnp.int32, (rows, rows), 1)
    if to_interleaved:
        row, col = col, row
    hit = col == (row % frames) * records + row // frames
    return hit.astype(F32).astype(BF16)


def head_pair(left, right, low):
    turned = pltpu.roll(jnp.where(low, right, left), HD, 1)
    return jnp.where(low, left, turned), jnp.where(low, turned, right)


def pack_kernel(
    grad_hbm,
    query_hbm,
    key_hbm,
    value_hbm,
    weight_hbm,
    sent_ref,
    grad_ref,
    query_ref,
    key_ref,
    value_ref,
    weight_ref,
    sems,
):
    frames, records, features = grad_ref.shape
    inner = weight_ref.shape[0]
    rows = frames * records
    loads = [
        pltpu.make_async_copy(source, target, sems.at[n])
        for n, (source, target) in enumerate(
            (
                (key_hbm, key_ref),
                (value_hbm, value_ref),
                (grad_hbm, grad_ref),
                (query_hbm, query_ref),
                (weight_hbm, weight_ref),
            )
        )
    ]
    for load in loads:
        load.start()
    order = one_hot_rows(rows, frames, records, False)

    def by_record(matrix):
        return jnp.dot(order, matrix, preferred_element_type=F32)

    low = low_half((frames, LANES))

    def place(first, second, start):
        for record in range(records):
            rs = slice(record * frames, (record + 1) * frames)
            for tile in range(inner // LANES):
                cs = slice(tile * LANES, (tile + 1) * LANES)
                pair = record * HEADS_W + 2 * tile
                sides = head_pair(first[rs, cs], second[rs, cs], low)
                for side in range(2):
                    sent_ref[pair + side, :, start : start + LANES] = sides[side].astype(BF16)

    loads[0].wait()
    loads[1].wait()
    key = by_record(key_ref[...].reshape(rows, inner))
    value = by_record(value_ref[...].reshape(rows, inner))
    place(key, value, LANES)
    loads[2].wait()
    flat_grad = by_record(grad_ref[...].reshape(rows, features)).astype(BF16)
    loads[3].wait()
    query = by_record(query_ref[...].reshape(rows, inner))
    loads[4].wait()
    heads_grad = lax.dot_general(
        flat_grad, weight_ref[...], NT, preferred_element_type=F32
    )
    place(query, heads_grad.astype(BF16).astype(F32), 0)


def attend_kernel(
    length_hbm,
    heads_ref,
    back_ref,
    kt_ref,
    gq_ref,
    bias_ref,
    terms_ref,
    prob_ref,
    acc_ref,
    length_ref,
    sem,
):
    load = pltpu.make_async_copy(length_hbm, length_ref, sem)
    load.start()
    length = heads_ref.shape[0]
    devices, packed, _ = back_ref.shape
    frames = length // devices
    block = terms_ref.shape[2]
    chunk = 128
    factor = HD ** (-0.5)
    rate = factor * LOG2E

    low = low_half((length, LANES))
    both = heads_ref[:, 0:LANES].astype(F32)
    only_g = jnp.where(low, 0.0, both).astype(BF16)
    only_q = jnp.where(low, both, 0.0).astype(BF16)
    for qb in range(length // block):
        rows = slice(qb * block, (qb + 1) * block)
        gq_ref[2 * qb * block : (2 * qb + 1) * block, :] = only_g[rows]
        gq_ref[(2 * qb + 1) * block : (2 * qb + 2) * block, :] = only_q[rows]
    kt_ref[...] = heads_ref[:, LANES:].astype(F32).T[0:HD].astype(BF16)
    load.wait()
    record = lax.axis_index("seq") // HEADS_W
    key_length = jnp.where(record == 0, length_ref[0, 0], length_ref[0, 1])
    bias_ref[...] = jnp.where(
        lax.broadcasted_iota(jnp.int32, (length, LANES), 0) < key_length, 0.0, MASKED
    )

    def fold(values, op):
        return op(values.reshape(-1, 8, block), axis=0)

    def first_stage(qb, c, state):
        ks = slice(c * chunk, (c + 1) * chunk)
        g_blk = gq_ref[2 * qb * block : (2 * qb + 1) * block, :]
        q_blk = gq_ref[(2 * qb + 1) * block : (2 * qb + 2) * block, :]
        bias = jnp.concatenate([bias_ref[ks, :]] * (block // LANES), axis=1)
        scores = (
            lax.dot_general(heads_ref[ks, LANES:], q_blk, NT, preferred_element_type=F32) + bias
        )
        peak = jnp.max(fold(scores, jnp.max), axis=0, keepdims=True)
        terms = jnp.exp2((scores - peak) * rate)
        grad_prob = lax.dot_general(
            heads_ref[ks, LANES:], g_blk, NT, preferred_element_type=F32
        )
        terms_ref[qb % 2, ks, :] = terms
        prob_ref[qb % 2, ks, :] = grad_prob
        state["peaks"].append(peak)
        state["sums"].append(fold(terms, jnp.sum))
        state["weighted"].append(fold(terms * grad_prob, jnp.sum))

    def row_totals(state):
        top = state["peaks"][0]
        for peak in state["peaks"][1:]:
            top = jnp.maximum(top, peak)
        scales = [jnp.exp2((peak - top) * rate) for peak in state["peaks"]]
        total = sum(part * scale for part, scale in zip(state["sums"], scales))
        weighted = sum(part * scale for part, scale in zip(state["weighted"], scales))
        share = 1.0 / jnp.sum(total, axis=0, keepdims=True)
        state["delta"] = jnp.sum(weighted, axis=0, keepdims=True) * share
        state["shares"] = [share * scale for scale in scales]
        state["grad_q"] = 0.0

    def last_stage(qb, c, state):
        ks = slice(c * chunk, (c + 1) * chunk)
        prob = terms_ref[qb % 2, ks, :] * state["shares"][c]
        grad_score = (prob * (prob_ref[qb % 2, ks, :] - state["delta"])).astype(BF16)
        update = jnp.dot(
            jnp.concatenate([prob.astype(BF16), grad_score], axis=1),
            gq_ref[2 * qb * block : (2 * qb + 2) * block, :],
            preferred_element_type=F32,
        )
        if qb == 0:
            acc_ref[ks, :] = update
        else:
            acc_ref[ks, :] += update
        state["grad_q"] = state["grad_q"] + jnp.dot(
            kt_ref[:, ks], grad_score, preferred_element_type=F32
        )

    def send_queries(qb, state):
        rows = (state["grad_q"].T * factor).reshape(block // frames, frames, HD)
        half = frames // 2
        for j in range(block // frames):
            back_ref[qb * (block // frames) + j, frames:packed, :] = jnp.concatenate(
                [rows[j, 0:half], rows[j, half:]], axis=1
            ).astype(BF16)

    blocks = length // block
    states = [dict(peaks=[], sums=[], weighted=[]) for _ in range(blocks)]
    for qb in range(blocks + 1):
        for c in range(length // chunk):
            if qb < blocks:
                first_stage(qb, c, states[qb])
            if qb > 0:
                last_stage(qb - 1, c, states[qb - 1])
        if qb < blocks:
            row_totals(states[qb])
        if qb > 0:
            send_queries(qb - 1, states[qb - 1])
    scale = jnp.where(low_half((1, LANES)), factor, 1.0)
    back_ref[:, 0:frames, :] = (acc_ref[...] * scale).astype(BF16).reshape(devices, frames, LANES)


def finish_kernel(back_ref, weight_ref, input_ref, grad_ref, gain_ref, out_ref, joined_ref):
    frames, records, features = grad_ref.shape
    rows = frames * records
    inner = weight_ref.shape[1] // 3
    half = frames // 2
    low = low_half((frames, LANES))
    low_part = low_half((half, LANES))
    for record in range(records):
        base = record * frames
        for tile in range(inner // LANES):
            pair = record * HEADS_W + 2 * tile
            first = back_ref[pair].astype(F32)
            second = back_ref[pair + 1].astype(F32)
            key, value = head_pair(first[0:frames], second[0:frames], low)
            upper, lower = head_pair(first[frames:], second[frames:], low_part)
            cs = tile * LANES
            joined_ref[base : base + half, cs : cs + LANES] = upper.astype(BF16)
            joined_ref[base + half : base + frames, cs : cs + LANES] = lower.astype(BF16)
            joined_ref[base : base + frames, inner + cs : inner + cs + LANES] = key.astype(BF16)
            joined_ref[base : base + frames, 2 * inner + cs : 2 * inner + cs + LANES] = (
                value.astype(BF16)
            )
    order = one_hot_rows(rows, frames, records, True)
    joined = jnp.dot(order, joined_ref[...], preferred_element_type=F32).astype(BF16)
    upstream = lax.dot_general(joined, weight_ref[...], NT, preferred_element_type=F32)
    inputs = input_ref[...].reshape(rows, features).astype(F32)
    row_mean = jnp.mean(inputs, axis=-1, keepdims=True)
    centred = inputs - row_mean
    row_var = jnp.mean(centred * centred, axis=-1, keepdims=True)
    inv_std = lax.rsqrt(row_var + 1e-05)
    normed = centred * inv_std
    scaled = upstream * gain_ref[...].astype(F32)
    branch = inv_std * (
        scaled
        - jnp.mean(scaled, axis=-1, keepdims=True)
        - normed * jnp.mean(scaled * normed, axis=-1, keepdims=True)
    )
    total = grad_ref[...].reshape(rows, features).astype(F32) + branch
    out_ref[...] = total.astype(BF16).reshape(frames, records, features)


def per_device(
    layer_input,
    grad_out,
    queries,
    keys_saved,
    values_saved,
    out_weight,
    qkv_weight,
    ln_gain,
    lengths,
):
    frames, records, features = grad_out.shape[1:]
    inner = out_weight.shape[1]
    devices = lax.axis_size("seq")
    length = devices * frames
    packed = frames + frames // 2
    block = 256
    vmem = pltpu.CompilerParams(vmem_limit_bytes=24 * 1024 * 1024)
    far = pl.BlockSpec(memory_space=pltpu.HBM)
    whole = pl.BlockSpec(memory_space=pltpu.VMEM)

    sent = pl.pallas_call(
        pack_kernel,
        out_shape=jax.ShapeDtypeStruct((devices, frames, 2 * LANES), BF16),
        in_specs=[far] * 5,
        out_specs=whole,
        scratch_shapes=[
            pltpu.VMEM((frames, records, features), BF16),
            pltpu.VMEM((frames, records, inner), BF16),
            pltpu.VMEM((frames, records, inner), BF16),
            pltpu.VMEM((frames, records, inner), BF16),
            pltpu.VMEM((inner, features), BF16),
            pltpu.SemaphoreType.DMA((5,)),
        ],
        compiler_params=vmem,
        name="pack",
    )(
        *(
            pltpu.with_memory_space_constraint(array[0], pltpu.HBM)
            for array in (grad_out, queries, keys_saved, values_saved, out_weight)
        )
    )
    heads = lax.all_to_all(sent, "seq", split_axis=0, concat_axis=0, tiled=True)
    back = pl.pallas_call(
        attend_kernel,
        out_shape=jax.ShapeDtypeStruct((devices, packed, LANES), BF16),
        in_specs=[far, whole],
        out_specs=whole,
        scratch_shapes=[
            pltpu.VMEM((HD, length), BF16),
            pltpu.VMEM((2 * length, LANES), BF16),
            pltpu.VMEM((length, LANES), F32),
            pltpu.VMEM((2, length, block), F32),
            pltpu.VMEM((2, length, block), F32),
            pltpu.VMEM((length, LANES), F32),
            pltpu.SMEM(lengths.shape, jnp.int32),
            pltpu.SemaphoreType.DMA,
        ],
        compiler_params=vmem,
        name="attend",
    )(pltpu.with_memory_space_constraint(lengths, pltpu.HBM), heads.reshape(length, 2 * LANES))
    back = lax.all_to_all(back, "seq", split_axis=0, concat_axis=0, tiled=True)
    total = pl.pallas_call(
        finish_kernel,
        out_shape=jax.ShapeDtypeStruct((frames, records, features), BF16),
        scratch_shapes=[pltpu.VMEM((frames * records, 3 * inner), BF16)],
        compiler_params=vmem,
        name="finish",
    )(back, qkv_weight[0], layer_input[0], grad_out[0], ln_gain)
    return passed_along(total, "pipe", -1)[None]


def solution(mesh):
    placed = (
        P("pipe", "seq", None, None),
        P("pipe", "seq", None, None),
        P("pipe", "seq", None, None),
        P("pipe", "seq", None, None),
        P("pipe", "seq", None, None),
        P("pipe", None, None),
        P("pipe", None, None),
        P("pipe", None),
        P("pipe", None),
    )
    return jax.shard_map(
        per_device,
        mesh=mesh,
        in_specs=placed,
        out_specs=P("pipe", "seq", None, None),
        check_vma=False,
    )
```

```python
import jax
import jax.numpy as jnp
from jax import lax
from jax.experimental import pallas as pl
from jax.experimental.pallas import tpu as pltpu
from jax.sharding import PartitionSpec as P

HEADS_W = 12
HD = 64
LANES = 128
MASKED = -1e30
LOG2E = 1.4426950408889634
F32 = jnp.float32
BF16 = jnp.bfloat16
NT = (((1,), (1,)), ((), ()))


def passed_along(block, axis, distance):
    devices = range(lax.axis_size(axis))
    route = [((i - distance) % len(devices), i) for i in devices]
    return lax.ppermute(block, axis, route)


def low_half(shape):
    return lax.broadcasted_iota(jnp.int32, shape, len(shape) - 1) < HD


def one_hot_rows(rows, frames, records, to_interleaved):
    row = lax.broadcasted_iota(jnp.int32, (rows, rows), 0)
    col = lax.broadcasted_iota(jnp.int32, (rows, rows), 1)
    if to_interleaved:
        row, col = col, row
    hit = col == (row % frames) * records + row // frames
    return hit.astype(F32).astype(BF16)


def head_pair(left, right, low):
    turned = pltpu.roll(jnp.where(low, right, left), HD, 1)
    return jnp.where(low, left, turned), jnp.where(low, turned, right)


def pack_kernel(
    grad_hbm,
    query_hbm,
    key_hbm,
    value_hbm,
    weight_hbm,
    sent_ref,
    grad_ref,
    query_ref,
    key_ref,
    value_ref,
    weight_ref,
    sems,
):
    frames, records, features = grad_ref.shape
    inner = weight_ref.shape[0]
    rows = frames * records
    loads = [
        pltpu.make_async_copy(source, target, sems.at[n])
        for n, (source, target) in enumerate(
            (
                (key_hbm, key_ref),
                (value_hbm, value_ref),
                (grad_hbm, grad_ref),
                (query_hbm, query_ref),
                (weight_hbm, weight_ref),
            )
        )
    ]
    for load in loads:
        load.start()
    order = one_hot_rows(rows, frames, records, False)

    def by_record(matrix):
        return jnp.dot(order, matrix, preferred_element_type=F32)

    low = low_half((frames, LANES))

    def place(first, second, start):
        for record in range(records):
            rs = slice(record * frames, (record + 1) * frames)
            for tile in range(inner // LANES):
                cs = slice(tile * LANES, (tile + 1) * LANES)
                pair = record * HEADS_W + 2 * tile
                sides = head_pair(first[rs, cs], second[rs, cs], low)
                for side in range(2):
                    sent_ref[pair + side, :, start : start + LANES] = sides[side].astype(BF16)

    loads[0].wait()
    loads[1].wait()
    key = by_record(key_ref[...].reshape(rows, inner))
    value = by_record(value_ref[...].reshape(rows, inner))
    place(key, value, LANES)
    loads[2].wait()
    flat_grad = by_record(grad_ref[...].reshape(rows, features)).astype(BF16)
    loads[3].wait()
    query = by_record(query_ref[...].reshape(rows, inner))
    loads[4].wait()
    heads_grad = lax.dot_general(
        flat_grad, weight_ref[...], NT, preferred_element_type=F32
    )
    place(query, heads_grad.astype(BF16).astype(F32), 0)


def attend_kernel(
    length_hbm,
    heads_ref,
    back_ref,
    kt_ref,
    gq_ref,
    bias_ref,
    terms_ref,
    prob_ref,
    acc_ref,
    length_ref,
    sem,
):
    load = pltpu.make_async_copy(length_hbm, length_ref, sem)
    load.start()
    length = heads_ref.shape[0]
    devices, packed, _ = back_ref.shape
    frames = length // devices
    block = terms_ref.shape[2]
    chunk = 128
    factor = HD ** (-0.5)
    rate = factor * LOG2E

    low = low_half((length, LANES))
    both = heads_ref[:, 0:LANES].astype(F32)
    only_g = jnp.where(low, 0.0, both).astype(BF16)
    only_q = jnp.where(low, both, 0.0).astype(BF16)
    for qb in range(length // block):
        rows = slice(qb * block, (qb + 1) * block)
        gq_ref[2 * qb * block : (2 * qb + 1) * block, :] = only_g[rows]
        gq_ref[(2 * qb + 1) * block : (2 * qb + 2) * block, :] = only_q[rows]
    kt_ref[...] = heads_ref[:, LANES:].astype(F32).T[0:HD].astype(BF16)
    load.wait()
    record = lax.axis_index("seq") // HEADS_W
    key_length = jnp.where(record == 0, length_ref[0, 0], length_ref[0, 1])
    bias_ref[...] = jnp.where(
        lax.broadcasted_iota(jnp.int32, (length, LANES), 0) < key_length, 0.0, MASKED
    )

    def fold(values, op):
        return op(values.reshape(-1, 8, block), axis=0)

    def first_stage(qb, c, state):
        ks = slice(c * chunk, (c + 1) * chunk)
        g_blk = gq_ref[2 * qb * block : (2 * qb + 1) * block, :]
        q_blk = gq_ref[(2 * qb + 1) * block : (2 * qb + 2) * block, :]
        bias = jnp.concatenate([bias_ref[ks, :]] * (block // LANES), axis=1)
        scores = (
            lax.dot_general(heads_ref[ks, LANES:], q_blk, NT, preferred_element_type=F32) + bias
        )
        peak = jnp.max(fold(scores, jnp.max), axis=0, keepdims=True)
        terms = jnp.exp2((scores - peak) * rate)
        grad_prob = lax.dot_general(
            heads_ref[ks, LANES:], g_blk, NT, preferred_element_type=F32
        )
        terms_ref[qb % 2, ks, :] = terms
        prob_ref[qb % 2, ks, :] = grad_prob
        state["peaks"].append(peak)
        state["sums"].append(fold(terms, jnp.sum))
        state["weighted"].append(fold(terms * grad_prob, jnp.sum))

    def row_totals(state):
        top = state["peaks"][0]
        for peak in state["peaks"][1:]:
            top = jnp.maximum(top, peak)
        scales = [jnp.exp2((peak - top) * rate) for peak in state["peaks"]]
        total = sum(part * scale for part, scale in zip(state["sums"], scales))
        weighted = sum(part * scale for part, scale in zip(state["weighted"], scales))
        share = 1.0 / jnp.sum(total, axis=0, keepdims=True)
        state["delta"] = jnp.sum(weighted, axis=0, keepdims=True) * share
        state["shares"] = [share * scale for scale in scales]
        state["grad_q"] = 0.0

    def last_stage(qb, c, state):
        ks = slice(c * chunk, (c + 1) * chunk)
        prob = terms_ref[qb % 2, ks, :] * state["shares"][c]
        grad_score = (prob * (prob_ref[qb % 2, ks, :] - state["delta"])).astype(BF16)
        update = jnp.dot(
            jnp.concatenate([prob.astype(BF16), grad_score], axis=1),
            gq_ref[2 * qb * block : (2 * qb + 2) * block, :],
            preferred_element_type=F32,
        )
        if qb == 0:
            acc_ref[ks, :] = update
        else:
            acc_ref[ks, :] += update
        state["grad_q"] = state["grad_q"] + jnp.dot(
            kt_ref[:, ks], grad_score, preferred_element_type=F32
        )

    def send_queries(qb, state):
        rows = (state["grad_q"].T * factor).reshape(block // frames, frames, HD)
        half = frames // 2
        for j in range(block // frames):
            back_ref[qb * (block // frames) + j, frames:packed, :] = jnp.concatenate(
                [rows[j, 0:half], rows[j, half:]], axis=1
            ).astype(BF16)

    blocks = length // block
    chunks = length // chunk

    def attend_to(used):
        states = [dict(peaks=[], sums=[], weighted=[]) for _ in range(blocks)]
        for qb in range(blocks + 1):
            for c in range(used):
                if qb < blocks:
                    first_stage(qb, c, states[qb])
                if qb > 0:
                    last_stage(qb - 1, c, states[qb - 1])
            if qb < blocks:
                row_totals(states[qb])
            if qb > 0:
                send_queries(qb - 1, states[qb - 1])
        scale = jnp.where(low_half((1, LANES)), factor, 1.0)
        full = used * chunk // frames
        back_ref[0:full, 0:frames, :] = (
            (acc_ref[0 : used * chunk, :] * scale).astype(BF16).reshape(full, frames, LANES)
        )
        if full < devices:
            back_ref[full:, 0:frames, :] = jnp.zeros((devices - full, frames, LANES), BF16)

    covered = 0
    for used in (chunks // 2, chunks * 2 // 3, chunks * 5 // 6, chunks):
        fits = key_length > covered * chunk
        if used < chunks:
            fits = jnp.logical_and(fits, key_length <= used * chunk)
        if covered == 0:
            fits = key_length <= used * chunk
        pl.when(fits)(lambda used=used: attend_to(used))
        covered = used


def finish_kernel(back_ref, weight_ref, input_ref, grad_ref, gain_ref, out_ref, joined_ref):
    frames, records, features = grad_ref.shape
    rows = frames * records
    inner = weight_ref.shape[1] // 3
    half = frames // 2
    low = low_half((frames, LANES))
    low_part = low_half((half, LANES))
    for record in range(records):
        base = record * frames
        for tile in range(inner // LANES):
            pair = record * HEADS_W + 2 * tile
            first = back_ref[pair].astype(F32)
            second = back_ref[pair + 1].astype(F32)
            key, value = head_pair(first[0:frames], second[0:frames], low)
            upper, lower = head_pair(first[frames:], second[frames:], low_part)
            cs = tile * LANES
            joined_ref[base : base + half, cs : cs + LANES] = upper.astype(BF16)
            joined_ref[base + half : base + frames, cs : cs + LANES] = lower.astype(BF16)
            joined_ref[base : base + frames, inner + cs : inner + cs + LANES] = key.astype(BF16)
            joined_ref[base : base + frames, 2 * inner + cs : 2 * inner + cs + LANES] = (
                value.astype(BF16)
            )
    order = one_hot_rows(rows, frames, records, True)
    joined = jnp.dot(order, joined_ref[...], preferred_element_type=F32).astype(BF16)
    upstream = lax.dot_general(joined, weight_ref[...], NT, preferred_element_type=F32)
    inputs = input_ref[...].reshape(rows, features).astype(F32)
    row_mean = jnp.mean(inputs, axis=-1, keepdims=True)
    centred = inputs - row_mean
    row_var = jnp.mean(centred * centred, axis=-1, keepdims=True)
    inv_std = lax.rsqrt(row_var + 1e-05)
    normed = centred * inv_std
    scaled = upstream * gain_ref[...].astype(F32)
    branch = inv_std * (
        scaled
        - jnp.mean(scaled, axis=-1, keepdims=True)
        - normed * jnp.mean(scaled * normed, axis=-1, keepdims=True)
    )
    total = grad_ref[...].reshape(rows, features).astype(F32) + branch
    out_ref[...] = total.astype(BF16).reshape(frames, records, features)


def per_device(
    layer_input,
    grad_out,
    queries,
    keys_saved,
    values_saved,
    out_weight,
    qkv_weight,
    ln_gain,
    lengths,
):
    frames, records, features = grad_out.shape[1:]
    inner = out_weight.shape[1]
    devices = lax.axis_size("seq")
    length = devices * frames
    packed = frames + frames // 2
    block = 256
    vmem = pltpu.CompilerParams(vmem_limit_bytes=24 * 1024 * 1024)
    far = pl.BlockSpec(memory_space=pltpu.HBM)
    whole = pl.BlockSpec(memory_space=pltpu.VMEM)

    sent = pl.pallas_call(
        pack_kernel,
        out_shape=jax.ShapeDtypeStruct((devices, frames, 2 * LANES), BF16),
        in_specs=[far] * 5,
        out_specs=whole,
        scratch_shapes=[
            pltpu.VMEM((frames, records, features), BF16),
            pltpu.VMEM((frames, records, inner), BF16),
            pltpu.VMEM((frames, records, inner), BF16),
            pltpu.VMEM((frames, records, inner), BF16),
            pltpu.VMEM((inner, features), BF16),
            pltpu.SemaphoreType.DMA((5,)),
        ],
        compiler_params=vmem,
        name="pack",
    )(
        *(
            pltpu.with_memory_space_constraint(array[0], pltpu.HBM)
            for array in (grad_out, queries, keys_saved, values_saved, out_weight)
        )
    )
    heads = lax.all_to_all(sent, "seq", split_axis=0, concat_axis=0, tiled=True)
    back = pl.pallas_call(
        attend_kernel,
        out_shape=jax.ShapeDtypeStruct((devices, packed, LANES), BF16),
        in_specs=[far, whole],
        out_specs=whole,
        scratch_shapes=[
            pltpu.VMEM((HD, length), BF16),
            pltpu.VMEM((2 * length, LANES), BF16),
            pltpu.VMEM((length, LANES), F32),
            pltpu.VMEM((2, length, block), F32),
            pltpu.VMEM((2, length, block), F32),
            pltpu.VMEM((length, LANES), F32),
            pltpu.SMEM(lengths.shape, jnp.int32),
            pltpu.SemaphoreType.DMA,
        ],
        compiler_params=vmem,
        name="attend",
    )(pltpu.with_memory_space_constraint(lengths, pltpu.HBM), heads.reshape(length, 2 * LANES))
    back = lax.all_to_all(back, "seq", split_axis=0, concat_axis=0, tiled=True)
    total = pl.pallas_call(
        finish_kernel,
        out_shape=jax.ShapeDtypeStruct((frames, records, features), BF16),
        scratch_shapes=[pltpu.VMEM((frames * records, 3 * inner), BF16)],
        compiler_params=vmem,
        name="finish",
    )(back, qkv_weight[0], layer_input[0], grad_out[0], ln_gain)
    return passed_along(total, "pipe", -1)[None]


def solution(mesh):
    placed = (
        P("pipe", "seq", None, None),
        P("pipe", "seq", None, None),
        P("pipe", "seq", None, None),
        P("pipe", "seq", None, None),
        P("pipe", "seq", None, None),
        P("pipe", None, None),
        P("pipe", None, None),
        P("pipe", None),
        P("pipe", None),
    )
    return jax.shard_map(
        per_device,
        mesh=mesh,
        in_specs=placed,
        out_specs=P("pipe", "seq", None, None),
        check_vma=False,
    )
```

```python
import jax
import jax.numpy as jnp
from jax import lax
from jax.experimental import pallas as pl
from jax.experimental.pallas import tpu as pltpu
from jax.sharding import PartitionSpec as P

HEADS_W = 12
HD = 64
LANES = 128
MASKED = -1e30
LOG2E = 1.4426950408889634
F32 = jnp.float32
BF16 = jnp.bfloat16
NT = (((1,), (1,)), ((), ()))


def passed_along(block, axis, distance):
    devices = range(lax.axis_size(axis))
    route = [((i - distance) % len(devices), i) for i in devices]
    return lax.ppermute(block, axis, route)


def low_half(shape):
    return lax.broadcasted_iota(jnp.int32, shape, len(shape) - 1) < HD


def one_hot_rows(rows, frames, records, to_interleaved):
    row = lax.broadcasted_iota(jnp.int32, (rows, rows), 0)
    col = lax.broadcasted_iota(jnp.int32, (rows, rows), 1)
    if to_interleaved:
        row, col = col, row
    hit = col == (row % frames) * records + row // frames
    return hit.astype(F32).astype(BF16)


def head_pair(left, right, low):
    turned = pltpu.roll(jnp.where(low, right, left), HD, 1)
    return jnp.where(low, left, turned), jnp.where(low, turned, right)


def pack_kernel(
    grad_hbm,
    query_hbm,
    key_hbm,
    value_hbm,
    weight_hbm,
    sent_ref,
    grad_ref,
    query_ref,
    key_ref,
    value_ref,
    weight_ref,
    sems,
):
    frames, records, features = grad_ref.shape
    inner = weight_ref.shape[0]
    rows = frames * records
    loads = [
        pltpu.make_async_copy(source, target, sems.at[n])
        for n, (source, target) in enumerate(
            (
                (key_hbm, key_ref),
                (value_hbm, value_ref),
                (grad_hbm, grad_ref),
                (query_hbm, query_ref),
                (weight_hbm, weight_ref),
            )
        )
    ]
    for load in loads:
        load.start()
    order = one_hot_rows(rows, frames, records, False)

    def by_record(matrix):
        return jnp.dot(order, matrix, preferred_element_type=F32)

    low = low_half((frames, LANES))

    def place(first, second, start):
        for record in range(records):
            rs = slice(record * frames, (record + 1) * frames)
            for tile in range(inner // LANES):
                cs = slice(tile * LANES, (tile + 1) * LANES)
                pair = record * HEADS_W + 2 * tile
                sides = head_pair(first[rs, cs], second[rs, cs], low)
                for side in range(2):
                    sent_ref[pair + side, :, start : start + LANES] = sides[side].astype(BF16)

    loads[0].wait()
    loads[1].wait()
    key = by_record(key_ref[...].reshape(rows, inner))
    value = by_record(value_ref[...].reshape(rows, inner))
    place(key, value, LANES)
    loads[2].wait()
    flat_grad = by_record(grad_ref[...].reshape(rows, features)).astype(BF16)
    loads[3].wait()
    query = by_record(query_ref[...].reshape(rows, inner))
    loads[4].wait()
    heads_grad = lax.dot_general(
        flat_grad, weight_ref[...], NT, preferred_element_type=F32
    )
    place(query, heads_grad.astype(BF16).astype(F32), 0)


def attend_kernel(
    length_hbm,
    heads_ref,
    back_ref,
    kt_ref,
    gq_ref,
    bias_ref,
    terms_ref,
    prob_ref,
    acc_ref,
    length_ref,
    sem,
):
    load = pltpu.make_async_copy(length_hbm, length_ref, sem)
    load.start()
    length = heads_ref.shape[0]
    devices, packed, _ = back_ref.shape
    frames = length // devices
    block = terms_ref.shape[2]
    chunk = 128
    factor = HD ** (-0.5)
    rate = factor * LOG2E

    low = low_half((length, LANES))
    both = heads_ref[:, 0:LANES].astype(F32)
    only_g = jnp.where(low, 0.0, both).astype(BF16)
    only_q = jnp.where(low, both, 0.0).astype(BF16)
    for qb in range(length // block):
        rows = slice(qb * block, (qb + 1) * block)
        gq_ref[2 * qb * block : (2 * qb + 1) * block, :] = only_g[rows]
        gq_ref[(2 * qb + 1) * block : (2 * qb + 2) * block, :] = only_q[rows]
    kt_ref[...] = heads_ref[:, LANES:].astype(F32).T[0:HD].astype(BF16)
    load.wait()
    record = lax.axis_index("seq") // HEADS_W
    key_length = jnp.where(record == 0, length_ref[0, 0], length_ref[0, 1])
    bias_ref[...] = jnp.where(
        lax.broadcasted_iota(jnp.int32, (length, LANES), 0) < key_length, 0.0, MASKED
    )

    def fold(values, op):
        return op(values.reshape(-1, 8, block), axis=0)

    def first_stage(qb, c, state):
        ks = slice(c * chunk, (c + 1) * chunk)
        g_blk = gq_ref[2 * qb * block : (2 * qb + 1) * block, :]
        q_blk = gq_ref[(2 * qb + 1) * block : (2 * qb + 2) * block, :]
        bias = jnp.concatenate([bias_ref[ks, :]] * (block // LANES), axis=1)
        scores = (
            lax.dot_general(heads_ref[ks, LANES:], q_blk, NT, preferred_element_type=F32) + bias
        )
        peak = jnp.max(fold(scores, jnp.max), axis=0, keepdims=True)
        terms = jnp.exp2((scores - peak) * rate)
        grad_prob = lax.dot_general(
            heads_ref[ks, LANES:], g_blk, NT, preferred_element_type=F32
        )
        terms_ref[qb % 2, ks, :] = terms
        prob_ref[qb % 2, ks, :] = grad_prob
        state["peaks"].append(peak)
        state["sums"].append(fold(terms, jnp.sum))
        state["weighted"].append(fold(terms * grad_prob, jnp.sum))

    def row_totals(state):
        top = state["peaks"][0]
        for peak in state["peaks"][1:]:
            top = jnp.maximum(top, peak)
        scales = [jnp.exp2((peak - top) * rate) for peak in state["peaks"]]
        total = sum(part * scale for part, scale in zip(state["sums"], scales))
        weighted = sum(part * scale for part, scale in zip(state["weighted"], scales))
        share = 1.0 / jnp.sum(total, axis=0, keepdims=True)
        state["delta"] = jnp.sum(weighted, axis=0, keepdims=True) * share
        state["shares"] = [share * scale for scale in scales]
        state["grad_q"] = 0.0

    def last_stage(qb, c, state):
        ks = slice(c * chunk, (c + 1) * chunk)
        prob = terms_ref[qb % 2, ks, :] * state["shares"][c]
        grad_score = (prob * (prob_ref[qb % 2, ks, :] - state["delta"])).astype(BF16)
        update = jnp.dot(
            jnp.concatenate([prob.astype(BF16), grad_score], axis=1),
            gq_ref[2 * qb * block : (2 * qb + 2) * block, :],
            preferred_element_type=F32,
        )
        if qb == 0:
            acc_ref[ks, :] = update
        else:
            acc_ref[ks, :] += update
        state["grad_q"] = state["grad_q"] + jnp.dot(
            kt_ref[:, ks], grad_score, preferred_element_type=F32
        )

    def send_queries(qb, state):
        rows = (state["grad_q"].T * factor).reshape(block // frames, frames, HD)
        half = frames // 2
        for j in range(block // frames):
            back_ref[qb * (block // frames) + j, frames:packed, :] = jnp.concatenate(
                [rows[j, 0:half], rows[j, half:]], axis=1
            ).astype(BF16)

    blocks = length // block
    chunks = length // chunk

    def attend_to(used):
        states = [dict(peaks=[], sums=[], weighted=[]) for _ in range(blocks)]
        for qb in range(blocks + 1):
            for c in range(used):
                if qb < blocks:
                    first_stage(qb, c, states[qb])
                if qb > 0:
                    last_stage(qb - 1, c, states[qb - 1])
            if qb < blocks:
                row_totals(states[qb])
            if qb > 0:
                send_queries(qb - 1, states[qb - 1])
        scale = jnp.where(low_half((1, LANES)), factor, 1.0)
        full = used * chunk // frames
        back_ref[0:full, 0:frames, :] = (
            (acc_ref[0 : used * chunk, :] * scale).astype(BF16).reshape(full, frames, LANES)
        )
        if full < devices:
            back_ref[full:, 0:frames, :] = jnp.zeros((devices - full, frames, LANES), BF16)

    covered = 0
    for used in (chunks * 2 // 3, chunks * 5 // 6, chunks * 11 // 12, chunks):
        fits = key_length > covered * chunk
        if used < chunks:
            fits = jnp.logical_and(fits, key_length <= used * chunk)
        if covered == 0:
            fits = key_length <= used * chunk
        pl.when(fits)(lambda used=used: attend_to(used))
        covered = used


def finish_kernel(back_ref, weight_ref, input_ref, grad_ref, gain_ref, out_ref, joined_ref):
    frames, records, features = grad_ref.shape
    rows = frames * records
    inner = weight_ref.shape[1] // 3
    half = frames // 2
    low = low_half((frames, LANES))
    low_part = low_half((half, LANES))
    for record in range(records):
        base = record * frames
        for tile in range(inner // LANES):
            pair = record * HEADS_W + 2 * tile
            first = back_ref[pair].astype(F32)
            second = back_ref[pair + 1].astype(F32)
            key, value = head_pair(first[0:frames], second[0:frames], low)
            upper, lower = head_pair(first[frames:], second[frames:], low_part)
            cs = tile * LANES
            joined_ref[base : base + half, cs : cs + LANES] = upper.astype(BF16)
            joined_ref[base + half : base + frames, cs : cs + LANES] = lower.astype(BF16)
            joined_ref[base : base + frames, inner + cs : inner + cs + LANES] = key.astype(BF16)
            joined_ref[base : base + frames, 2 * inner + cs : 2 * inner + cs + LANES] = (
                value.astype(BF16)
            )
    order = one_hot_rows(rows, frames, records, True)
    joined = jnp.dot(order, joined_ref[...], preferred_element_type=F32).astype(BF16)
    upstream = lax.dot_general(joined, weight_ref[...], NT, preferred_element_type=F32)
    inputs = input_ref[...].reshape(rows, features).astype(F32)
    row_mean = jnp.mean(inputs, axis=-1, keepdims=True)
    centred = inputs - row_mean
    row_var = jnp.mean(centred * centred, axis=-1, keepdims=True)
    inv_std = lax.rsqrt(row_var + 1e-05)
    normed = centred * inv_std
    scaled = upstream * gain_ref[...].astype(F32)
    branch = inv_std * (
        scaled
        - jnp.mean(scaled, axis=-1, keepdims=True)
        - normed * jnp.mean(scaled * normed, axis=-1, keepdims=True)
    )
    total = grad_ref[...].reshape(rows, features).astype(F32) + branch
    out_ref[...] = total.astype(BF16).reshape(frames, records, features)


def per_device(
    layer_input,
    grad_out,
    queries,
    keys_saved,
    values_saved,
    out_weight,
    qkv_weight,
    ln_gain,
    lengths,
):
    frames, records, features = grad_out.shape[1:]
    inner = out_weight.shape[1]
    devices = lax.axis_size("seq")
    length = devices * frames
    packed = frames + frames // 2
    block = 256
    vmem = pltpu.CompilerParams(vmem_limit_bytes=24 * 1024 * 1024)
    far = pl.BlockSpec(memory_space=pltpu.HBM)
    whole = pl.BlockSpec(memory_space=pltpu.VMEM)

    sent = pl.pallas_call(
        pack_kernel,
        out_shape=jax.ShapeDtypeStruct((devices, frames, 2 * LANES), BF16),
        in_specs=[far] * 5,
        out_specs=whole,
        scratch_shapes=[
            pltpu.VMEM((frames, records, features), BF16),
            pltpu.VMEM((frames, records, inner), BF16),
            pltpu.VMEM((frames, records, inner), BF16),
            pltpu.VMEM((frames, records, inner), BF16),
            pltpu.VMEM((inner, features), BF16),
            pltpu.SemaphoreType.DMA((5,)),
        ],
        compiler_params=vmem,
        name="pack",
    )(
        *(
            pltpu.with_memory_space_constraint(array[0], pltpu.HBM)
            for array in (grad_out, queries, keys_saved, values_saved, out_weight)
        )
    )
    heads = lax.all_to_all(sent, "seq", split_axis=0, concat_axis=0, tiled=True)
    back = pl.pallas_call(
        attend_kernel,
        out_shape=jax.ShapeDtypeStruct((devices, packed, LANES), BF16),
        in_specs=[far, whole],
        out_specs=whole,
        scratch_shapes=[
            pltpu.VMEM((HD, length), BF16),
            pltpu.VMEM((2 * length, LANES), BF16),
            pltpu.VMEM((length, LANES), F32),
            pltpu.VMEM((2, length, block), F32),
            pltpu.VMEM((2, length, block), F32),
            pltpu.VMEM((length, LANES), F32),
            pltpu.SMEM(lengths.shape, jnp.int32),
            pltpu.SemaphoreType.DMA,
        ],
        compiler_params=vmem,
        name="attend",
    )(pltpu.with_memory_space_constraint(lengths, pltpu.HBM), heads.reshape(length, 2 * LANES))
    back = lax.all_to_all(back, "seq", split_axis=0, concat_axis=0, tiled=True)
    total = pl.pallas_call(
        finish_kernel,
        out_shape=jax.ShapeDtypeStruct((frames, records, features), BF16),
        scratch_shapes=[pltpu.VMEM((frames * records, 3 * inner), BF16)],
        compiler_params=vmem,
        name="finish",
    )(back, qkv_weight[0], layer_input[0], grad_out[0], ln_gain)
    return passed_along(total, "pipe", -1)[None]


def solution(mesh):
    placed = (
        P("pipe", "seq", None, None),
        P("pipe", "seq", None, None),
        P("pipe", "seq", None, None),
        P("pipe", "seq", None, None),
        P("pipe", "seq", None, None),
        P("pipe", None, None),
        P("pipe", None, None),
        P("pipe", None),
        P("pipe", None),
    )
    return jax.shard_map(
        per_device,
        mesh=mesh,
        in_specs=placed,
        out_specs=P("pipe", "seq", None, None),
        check_vma=False,
    )
```
